32 devices in a mesh: seq: 16 (over z, y, core), head: 2 (over x).
Axes of the slice: x: 2, y: 2, z: 4, core: 2. Of those that a mesh axis runs over, the one named last changes fastest.
Arguments:
- q_nope: bfloat16 [4096, 8192], P('seq', 'head'), may hold values from -6 to 6
- q_rope: bfloat16 [4096, 4096], P('seq', 'head'), may hold values from -8 to 8
- latent: bfloat16 [4096, 576], P('seq'), may hold values from -8 to 8
- doc_ids: int32 [4096], P('seq'), may hold values from 0 to 15, never falling along the last dimension, each value on 1 to 1280 neighbouring positions
- w_uk: bfloat16 [512, 8192], P(None, 'head'), may hold values from -0.25 to 0.25
- w_uv: bfloat16 [512, 8192], P(None, 'head'), may hold values from -0.25 to 0.25
- w_out: bfloat16 [8192, 3584], P('head', 'seq'), may hold values from -0.375 to 0.375
Outputs:
- projected: bfloat16 [4096, 3584], P('seq', 'head')
The draws below stay inside these ranges and needn't reach their ends.
Inputs may be any that keep to these rules, and one draw needn't show every extreme that they name: `doc_ids`: document ids never fall along the sequence; every document holds 1 to 1280 tokens, and one holds exactly that many.
All inputs are finite; a program needn't handle non-finite values.
Results may differ from the reference program's by a relative error of at most 0.0065.
Values may be sent and summed in bfloat16 or wider, within the bound.
A program may use at most 128 MiB of HBM per device.

```python
import math
import jax
import jax.numpy as jnp
import numpy as np
from jax import lax

HD = 128
ROPE = 64
VD = 128
LAT = 512
HEADS = 64
DOUT = 3584
HOPS = 4
TOK_DEV = 256
TOKENS = 4096
N_SEQ = 16


def rope_parts(key):
    base_key = jax.random.fold_in(key, 101)
    key_one, key_two = jax.random.split(base_key, 2)
    key_rows = jnp.clip(jax.random.normal(key_one, (TOKENS, ROPE), jnp.float32), -8.0, 8.0)
    queries = jnp.clip(jax.random.normal(key_two, (TOKENS, HEADS, ROPE), jnp.float32), -8.0, 8.0)
    return (key_rows, queries.reshape(TOKENS, HEADS * ROPE))


def draw_latent(key, part):
    key_rows, unused_queries = rope_parts(key)
    content_key = jax.random.fold_in(key, 202)
    content = jnp.clip(jax.random.normal(content_key, (TOKENS, LAT), jnp.float32), -8.0, 8.0)
    return jnp.concatenate([content, key_rows], axis=1).astype(jnp.bfloat16)


def draw_q_rope(key, part):
    return rope_parts(key)[1].astype(jnp.bfloat16)


def steps_of(own_key, extent, cuts, smallest, high):
    level, own = 1.0, jax.random.fold_in(own_key, 6)
    for axis_at, shards_of in cuts:
        draws = jnp.exp(jax.random.uniform(jax.random.fold_in(own, axis_at), (shards_of,), jnp.float32, smallest / len(cuts), high / len(cuts)))
        level = level * jnp.repeat(draws, extent[axis_at] // shards_of).reshape([-1 if axis == axis_at else 1 for axis in range(len(extent))])
    return level


def split_up(count, total, bound, slope):
    weights = [(1 << 20) // math.isqrt(standing ** slope) + 1 for standing in range(2, count + 1)]
    spare, given = total - bound - (count - 1), [1] * (count - 1)
    while spare > 0:
        movable = [i for i in range(count - 1) if given[i] < bound]
        pool, remaining = sum([weights[i] for i in movable]), spare
        for i in movable:
            extra = min(bound - given[i], max(1, remaining * weights[i] // pool), spare)
            given[i] = given[i] + extra
            spare = spare - extra
    return np.array([bound] + given)


def uneven(own_key, count, total, bound, lean):
    if count == 2:
        one = jax.random.randint(own_key, (), max(1, total - bound), min(bound, total - 1) + 1)
        return jnp.stack([one, total - one])
    sizes = jnp.asarray(split_up(count, total, bound, lean), jnp.int32)
    twos = (count - 1) // 2
    giver, sink = sizes[1:1 + 2 * twos:2], sizes[2:2 + 2 * twos:2]
    room = jnp.minimum(giver - 1, bound - sink)
    passed = jax.random.randint(jax.random.fold_in(own_key, 1), (twos,), 0, 1 << 20) % (room + 1)
    sizes = sizes.at[1:1 + 2 * twos:2].set(giver - passed).at[2:2 + 2 * twos:2].set(sink + passed)
    return sizes[jax.random.permutation(jax.random.fold_in(own_key, 2), count)]


def gaussian(own_key, shape, spread, bound, cuts=(), kind=jnp.bfloat16):
    entries = jax.random.normal(own_key, shape, jnp.float32) * spread
    if len(cuts) > 0:
        entries = steps_of(own_key, shape, cuts, -0.22, 0.18) * entries
    return jnp.clip(entries, min=-bound, max=bound).astype(kind)


def setup_inputs(seed: int = 0) -> dict:
    keys = jax.random.split(jax.random.key(seed), 8)
    q_nope = gaussian(keys[0], (TOKENS, HEADS * HD), 1.0, 6.0, ((0, 16), (1, 2)))
    q_rope = draw_q_rope(jax.random.fold_in(keys[7], 71), 0)
    latent = draw_latent(jax.random.fold_in(keys[7], 71), 0)
    doc_ids = jnp.searchsorted(jnp.cumsum(uneven(keys[3], N_SEQ, TOKENS, (HOPS + 1) * TOK_DEV, 2)), jnp.arange(TOKENS), side="right").astype(jnp.int32)
    w_uk = gaussian(keys[4], (LAT, HEADS * HD), LAT ** -0.5, 0.25, ((1, 2),))
    w_uv = gaussian(keys[5], (LAT, HEADS * VD), LAT ** -0.5, 0.25, ((1, 2),))
    w_out = gaussian(keys[6], (HEADS * VD, DOUT), (HEADS * VD // 32) ** -0.5, 0.375, ((0, 2), (1, 16)))
    return dict(q_nope=q_nope, q_rope=q_rope, latent=latent, doc_ids=doc_ids, w_uk=w_uk, w_uv=w_uv, w_out=w_out)


def reference(q_nope, q_rope, latent, doc_ids, w_uk, w_uv, w_out):
    score_scale = 1.0 / math.sqrt(HD + ROPE)
    content = latent[:, :LAT]
    key_nope = jnp.dot(content, w_uk, preferred_element_type=jnp.float32).astype(jnp.bfloat16)
    values = jnp.dot(content, w_uv, preferred_element_type=jnp.float32).astype(jnp.bfloat16)
    key_rope = latent[:, LAT:]
    reach_back = HOPS * TOK_DEV
    key_span = (HOPS + 1) * TOK_DEV
    nope_padded = jnp.pad(key_nope, ((reach_back, 0), (0, 0)))
    rope_padded = jnp.pad(key_rope, ((reach_back, 0), (0, 0)))
    value_padded = jnp.pad(values, ((reach_back, 0), (0, 0)))
    doc_padded = jnp.pad(doc_ids, (reach_back, 0), constant_values=-1)

    def one_block(block_index):
        offset = (block_index * TOK_DEV).astype(jnp.int32)
        query_nope = lax.dynamic_slice_in_dim(q_nope, offset, TOK_DEV, 0).astype(jnp.float32).reshape(TOK_DEV, HEADS, HD)
        query_rope = lax.dynamic_slice_in_dim(q_rope, offset, TOK_DEV, 0).astype(jnp.float32).reshape(TOK_DEV, HEADS, ROPE)
        block_nope = lax.dynamic_slice_in_dim(nope_padded, offset, key_span, 0).astype(jnp.float32).reshape(key_span, HEADS, HD)
        block_rope = lax.dynamic_slice_in_dim(rope_padded, offset, key_span, 0).astype(jnp.float32)
        block_values = lax.dynamic_slice_in_dim(value_padded, offset, key_span, 0).astype(jnp.float32).reshape(key_span, HEADS, VD)
        query_doc = lax.dynamic_slice_in_dim(doc_ids, offset, TOK_DEV, 0)
        key_doc = lax.dynamic_slice_in_dim(doc_padded, offset, key_span, 0)
        query_pos = offset + jnp.arange(TOK_DEV, dtype=jnp.int32)
        key_pos = offset - reach_back + jnp.arange(key_span, dtype=jnp.int32)
        distance = query_pos[:, None] - key_pos[None, :]
        allowed = (key_pos[None, :] >= 0) & (distance >= 0) & (distance < reach_back) & (query_doc[:, None] == key_doc[None, :])
        scores = (jnp.einsum('qhd,khd->hqk', query_nope, block_nope) + jnp.einsum('qhd,kd->hqk', query_rope, block_rope)) * score_scale
        scores = jnp.where(allowed[None], scores, jnp.float32(-1e+30))
        row_max = lax.optimization_barrier(jnp.max(scores, axis=-1, keepdims=True))
        raw_weights = jnp.where(allowed[None], jnp.exp(scores - row_max), jnp.float32(0.0))
        weights_half = (raw_weights / lax.optimization_barrier(jnp.sum(raw_weights, axis=-1, keepdims=True))).astype(jnp.bfloat16)
        attended = jnp.einsum('hqk,khd->qhd', weights_half.astype(jnp.float32), block_values)
        return attended.astype(jnp.bfloat16).reshape(TOK_DEV, HEADS * VD)
    blocks = lax.map(one_block, jnp.arange(N_SEQ, dtype=jnp.int32))
    attended_all = blocks.reshape(TOKENS, HEADS * VD)
    return jnp.dot(attended_all, w_out, preferred_element_type=jnp.float32).astype(jnp.bfloat16)
```

```python
import functools
import math

import jax
import jax.numpy as jnp
from jax import lax
from jax.experimental import pallas as pl
from jax.experimental.pallas import tpu as pltpu
from jax.sharding import PartitionSpec as P

HD = 128
ROPE = 64
VD = 128
LAT = 512
HOPS = 4
MARKS = 64
FAR = 1e30
PIECES = 2


def from_behind(value, steps):
    count = lax.axis_size("seq")
    return lax.ppermute(value, "seq", [(source, source + steps) for source in range(count - steps)])


def attend(rows, q_nope, q_rope, q_mark, content, tails, w_uk, w_uv, out):
    scale = math.log2(math.e) / math.sqrt(HD + ROPE)
    keys = content.shape[0]
    key_pair = jnp.dot(content[...], w_uk[...], preferred_element_type=jnp.float32).astype(jnp.bfloat16)
    value_pair = jnp.dot(content[...], w_uv[...], preferred_element_type=jnp.float32).astype(jnp.bfloat16)
    causal = lax.broadcasted_iota(jnp.int32, (rows, rows), 1) <= lax.broadcasted_iota(jnp.int32, (rows, rows), 0)
    low = lax.broadcasted_iota(jnp.int32, (rows, 2 * ROPE), 1) < ROPE
    ones = jnp.ones((keys, VD), jnp.bfloat16)
    for half in range(2):
        cols = slice(half * HD, (half + 1) * HD)
        rope = jnp.where(low == (half == 0), q_rope[...], q_mark[...])
        query = jnp.concatenate([q_nope[:, cols], rope], axis=1)
        key = jnp.concatenate([key_pair[:, cols], tails[half]], axis=1)
        scores = lax.dot_general(query, key, (((1,), (1,)), ((), ())), preferred_element_type=jnp.float32)
        edge = jnp.where(causal, scores[:, keys - rows :], scores[:, :rows])
        joined = jnp.concatenate([edge, scores[:, rows : keys - rows]], axis=1)
        top = jnp.max(joined, axis=-1, keepdims=True)
        raw = jnp.exp2((joined - top) * scale).astype(jnp.bfloat16)
        near = jnp.where(causal, raw[:, :rows], jnp.bfloat16(0))
        far = jnp.where(causal, jnp.bfloat16(0), raw[:, :rows])
        weights = jnp.concatenate([far, raw[:, rows:], near], axis=1)
        value = jnp.concatenate([value_pair[:, cols], ones], axis=1)
        total = jnp.dot(weights, value, preferred_element_type=jnp.float32)
        out[:, cols] = (total[:, :VD] / total[:, VD:]).astype(jnp.bfloat16)


def attention(q_nope, q_rope, q_mark, content, tails, w_uk, w_uv):
    rows, width = q_nope.shape
    keys = content.shape[0]
    pairs = width // (2 * HD)
    whole = lambda *shape: pl.BlockSpec(shape, lambda i: (0,) * len(shape))
    return pl.pallas_call(
        functools.partial(attend, rows),
        out_shape=jax.ShapeDtypeStruct((rows, width), jnp.bfloat16),
        grid=(pairs,),
        in_specs=[
            pl.BlockSpec((rows, 2 * HD), lambda i: (0, i)),
            pl.BlockSpec((rows, 2 * ROPE), lambda i: (0, i)),
            whole(rows, 2 * ROPE),
            whole(keys, LAT),
            whole(2, keys, 2 * ROPE),
            pl.BlockSpec((LAT, 2 * HD), lambda i: (0, i)),
            pl.BlockSpec((LAT, 2 * HD), lambda i: (0, i)),
        ],
        out_specs=pl.BlockSpec((rows, 2 * VD), lambda i: (0, i)),
        compiler_params=pltpu.CompilerParams(
            dimension_semantics=("arbitrary",), vmem_limit_bytes=48 << 20
        ),
        cost_estimate=pl.CostEstimate(
            flops=pairs * 2 * keys * (2 * LAT * 2 * HD + 4 * rows * 2 * HD),
            bytes_accessed=2 * (rows * width * 3 + LAT * width * 2),
            transcendentals=pairs * 2 * rows * keys,
        ),
        name="attention",
    )(q_nope, q_rope, q_mark, content, tails, w_uk, w_uv)


def shards(q_nope, q_rope, latent, doc_ids, w_uk, w_uv, w_out):
    rows = q_nope.shape[0]
    count = lax.axis_size("seq")
    position = lax.axis_index("seq")
    w_rows = w_out.T
    step = w_rows.shape[0] // PIECES
    gathered = [
        lax.all_gather(w_rows[i * step : (i + 1) * step], "seq", axis=0, tiled=True)
        for i in range(PIECES)
    ]
    marks = (doc_ids[:, None] == jnp.arange(MARKS, dtype=jnp.int32)[None, :]).astype(jnp.bfloat16)
    payload = jnp.concatenate([latent, marks], axis=1)
    blocks = []
    for distance in range(HOPS, 0, -1):
        block = from_behind(payload, distance)
        blocks.append(
            jnp.concatenate(
                [block[:, : LAT + ROPE], jnp.where(position >= distance, block[:, LAT + ROPE :], jnp.bfloat16(1))],
                axis=1,
            )
        )
    blocks.append(payload)
    behind = jnp.concatenate(blocks, axis=0)
    content = behind[:, :LAT]
    key_rope, key_marks = behind[:, LAT : LAT + ROPE], behind[:, LAT + ROPE :]
    tails = jnp.stack(
        [jnp.concatenate([key_rope, key_marks], axis=1), jnp.concatenate([key_marks, key_rope], axis=1)]
    )
    q_mark = (marks - jnp.bfloat16(1)) * jnp.bfloat16(FAR)
    q_mark = jnp.concatenate([q_mark, q_mark], axis=1)
    attended = attention(q_nope, q_rope, q_mark, content, tails, w_uk, w_uv)
    heads = lax.axis_size("head")
    mine = lax.axis_index("head")
    swap = [(a, b) for a in range(heads) for b in range(heads) if a != b]
    parts = []
    for piece in gathered:
        share = lax.dot_general(
            attended, piece, (((1,), (1,)), ((), ())), preferred_element_type=jnp.float32
        )
        parts.append(lax.psum_scatter(share, "head", scatter_dimension=1, tiled=True) if heads > 2 else exchange(share, mine))
    joined = jnp.stack([part.reshape(rows, count // heads, step) for part in parts], axis=2)
    return joined.reshape(rows, -1).astype(jnp.bfloat16)


def exchange(share, mine):
    half = share.shape[1] // 2
    first, second = share[:, :half], share[:, half:]
    keep = jnp.where(mine == 0, first, second)
    give = jnp.where(mine == 0, second, first).astype(jnp.bfloat16)
    return keep + lax.ppermute(give, "head", [(0, 1), (1, 0)]).astype(jnp.float32)


def solution(mesh):
    placed = (
        P("seq", "head"),
        P("seq", "head"),
        P("seq", None),
        P("seq"),
        P(None, "head"),
        P(None, "head"),
        P("head", "seq"),
    )
    return jax.shard_map(
        shards, mesh=mesh, in_specs=placed, out_specs=P("seq", "head"), check_vma=False
    )
```

```python
import functools
import math

import jax
import jax.numpy as jnp
from jax import lax
from jax.experimental import pallas as pl
from jax.experimental.pallas import tpu as pltpu
from jax.sharding import PartitionSpec as P

HD = 128
ROPE = 64
VD = 128
LAT = 512
HOPS = 4
MARKS = 64
FAR = 1e30
PIECES = 2
PLANE = 4
PARTS = 2


def from_behind(value, steps):
    count = lax.axis_size("seq")
    return lax.ppermute(value, "seq", [(source, source + steps) for source in range(count - steps)])


def attend(rows, q_nope, q_rope, q_mark, content, tails, w_uk, w_uv, out):
    scale = math.log2(math.e) / math.sqrt(HD + ROPE)
    keys = content.shape[0]
    key_pair = jnp.dot(content[...], w_uk[...], preferred_element_type=jnp.float32).astype(jnp.bfloat16)
    value_pair = jnp.dot(content[...], w_uv[...], preferred_element_type=jnp.float32).astype(jnp.bfloat16)
    causal = lax.broadcasted_iota(jnp.int32, (rows, rows), 1) <= lax.broadcasted_iota(jnp.int32, (rows, rows), 0)
    low = lax.broadcasted_iota(jnp.int32, (rows, 2 * ROPE), 1) < ROPE
    ones = jnp.ones((keys, VD), jnp.bfloat16)
    for half in range(2):
        cols = slice(half * HD, (half + 1) * HD)
        rope = jnp.where(low == (half == 0), q_rope[...], q_mark[...])
        query = jnp.concatenate([q_nope[:, cols], rope], axis=1)
        key = jnp.concatenate([key_pair[:, cols], tails[half]], axis=1)
        scores = lax.dot_general(query, key, (((1,), (1,)), ((), ())), preferred_element_type=jnp.float32)
        edge = jnp.where(causal, scores[:, keys - rows :], scores[:, :rows])
        joined = jnp.concatenate([edge, scores[:, rows : keys - rows]], axis=1)
        top = jnp.max(joined, axis=-1, keepdims=True)
        raw = jnp.exp2((joined - top) * scale).astype(jnp.bfloat16)
        near = jnp.where(causal, raw[:, :rows], jnp.bfloat16(0))
        far = jnp.where(causal, jnp.bfloat16(0), raw[:, :rows])
        weights = jnp.concatenate([far, raw[:, rows:], near], axis=1)
        value = jnp.concatenate([value_pair[:, cols], ones], axis=1)
        total = jnp.dot(weights, value, preferred_element_type=jnp.float32)
        out[:, cols] = (total[:, :VD] / total[:, VD:]).astype(jnp.bfloat16)


def attention(q_nope, q_rope, q_mark, content, tails, w_uk, w_uv):
    rows, width = q_nope.shape
    keys = content.shape[0]
    pairs = width // (2 * HD)
    whole = lambda *shape: pl.BlockSpec(shape, lambda i: (0,) * len(shape))
    return pl.pallas_call(
        functools.partial(attend, rows),
        out_shape=jax.ShapeDtypeStruct((rows, width), jnp.bfloat16),
        grid=(pairs,),
        in_specs=[
            pl.BlockSpec((rows, 2 * HD), lambda i: (0, i)),
            pl.BlockSpec((rows, 2 * ROPE), lambda i: (0, i)),
            whole(rows, 2 * ROPE),
            whole(keys, LAT),
            whole(2, keys, 2 * ROPE),
            pl.BlockSpec((LAT, 2 * HD), lambda i: (0, i)),
            pl.BlockSpec((LAT, 2 * HD), lambda i: (0, i)),
        ],
        out_specs=pl.BlockSpec((rows, 2 * VD), lambda i: (0, i)),
        compiler_params=pltpu.CompilerParams(
            dimension_semantics=("arbitrary",), vmem_limit_bytes=48 << 20
        ),
        cost_estimate=pl.CostEstimate(
            flops=pairs * 2 * keys * (2 * LAT * 2 * HD + 4 * rows * 2 * HD),
            bytes_accessed=2 * (rows * width * 3 + LAT * width * 2),
            transcendentals=pairs * 2 * rows * keys,
        ),
        name="attention",
    )(q_nope, q_rope, q_mark, content, tails, w_uk, w_uv)


def shards(q_nope, q_rope, latent, doc_ids, w_uk, w_uv, w_out):
    count, heads = lax.axis_size("seq"), lax.axis_size("head")
    position = lax.axis_index("seq")
    w_rows = w_out.T
    marks = (doc_ids[:, None] == jnp.arange(MARKS, dtype=jnp.int32)[None, :]).astype(jnp.bfloat16)
    payload = jnp.concatenate([latent, marks], axis=1)
    blocks = []
    for distance in range(HOPS, 0, -1):
        block = from_behind(payload, distance)
        blocks.append(
            jnp.concatenate(
                [block[:, : LAT + ROPE], jnp.where(position >= distance, block[:, LAT + ROPE :], jnp.bfloat16(1))],
                axis=1,
            )
        )
    blocks.append(payload)
    behind = jnp.concatenate(blocks, axis=0)
    content = behind[:, :LAT]
    key_rope, key_marks = behind[:, LAT : LAT + ROPE], behind[:, LAT + ROPE :]
    tails = jnp.stack(
        [jnp.concatenate([key_rope, key_marks], axis=1), jnp.concatenate([key_marks, key_rope], axis=1)]
    )
    q_mark = (marks - jnp.bfloat16(1)) * jnp.bfloat16(FAR)
    q_mark = jnp.concatenate([q_mark, q_mark], axis=1)
    fixed = (q_mark, content, tails)
    if count == 4 * PLANE and heads == 2:
        return paired(w_rows, q_nope, q_rope, fixed, w_uk, w_uv)
    attended = attention(q_nope, q_rope, *fixed, w_uk, w_uv)
    whole = lax.all_gather(w_rows, "seq", axis=0, tiled=True)
    share = product(attended, whole)
    return lax.psum_scatter(share, "head", scatter_dimension=1, tiled=True).astype(jnp.bfloat16)


def product(left, right):
    return lax.dot_general(left, right, (((1,), (1,)), ((), ())), preferred_element_type=jnp.float32)


def swapped(value, bit):
    return lax.ppermute(value, "seq", [(i, i ^ bit) for i in range(lax.axis_size("seq"))])


def spread(block, rank):
    across = swapped(block, 2)
    two = jnp.stack([block, across])
    other = swapped(two, 1)
    first = jnp.where(rank % 2 == 0, two, other)
    second = jnp.where(rank % 2 == 0, other, two)
    here, there = (first[0], second[0]), (first[1], second[1])
    low = rank < 2
    return jnp.concatenate(
        [jnp.where(low, h, t) for h, t in zip(here, there)] + [jnp.where(low, t, h) for h, t in zip(here, there)], axis=0
    )


def to_owner(share, near):
    pairs = []
    for seq in range(lax.axis_size("seq")):
        group = seq // (2 * PLANE)
        keeper = group if near else 1 - group
        pairs.append((2 * seq + 1 - keeper, 2 * seq + keeper))
    return lax.ppermute(share.astype(jnp.bfloat16), ("seq", "head"), pairs).astype(jnp.float32)


def paired(w_rows, q_nope, q_rope, fixed, w_uk, w_uv):
    rows, width = q_nope.shape
    position, mine = lax.axis_index("seq"), lax.axis_index("head")
    plane, rank = position // PLANE, position % PLANE
    slab = w_rows.shape[0]
    step = slab // PIECES
    near = spread(w_rows, rank)
    far = [
        spread(swapped(w_rows[i * step : (i + 1) * step], 2 * PLANE), rank) for i in range(PIECES)
    ]
    own, partner = [], []
    for i in range(PARTS):
        cut = width // PARTS
        part = attention(
            q_nope[:, i * cut : (i + 1) * cut],
            q_rope[:, i * cut // 2 : (i + 1) * cut // 2],
            *fixed,
            w_uk[:, i * cut : (i + 1) * cut],
            w_uv[:, i * cut : (i + 1) * cut],
        )
        own.append(part)
        partner.append(swapped(part, PLANE))
    own, partner = jnp.concatenate(own, axis=1), jnp.concatenate(partner, axis=1)
    keeps_near = plane // 2 == mine

    def finish(tokens):
        share = product(tokens, near)
        near_sum = share + to_owner(share, True)
        far_sums = []
        for piece in far:
            share = product(tokens, piece)
            far_sums.append((share + to_owner(share, False)).reshape(rows, PLANE, step))
        far_sum = jnp.stack(far_sums, axis=2).reshape(rows, PLANE * slab)
        return jnp.where(keeps_near, near_sum, far_sum).astype(jnp.bfloat16)

    back = swapped(finish(partner), PLANE)
    here = finish(own)
    even = plane % 2 == 0
    return jnp.concatenate([jnp.where(even, here, back), jnp.where(even, back, here)], axis=1)


def solution(mesh):
    placed = (
        P("seq", "head"),
        P("seq", "head"),
        P("seq", None),
        P("seq"),
        P(None, "head"),
        P(None, "head"),
        P("head", "seq"),
    )
    return jax.shard_map(
        shards, mesh=mesh, in_specs=placed, out_specs=P("seq", "head"), check_vma=False
    )
```

```python
import functools
import math

import jax
import jax.numpy as jnp
from jax import lax
from jax.experimental import pallas as pl
from jax.experimental.pallas import tpu as pltpu
from jax.sharding import PartitionSpec as P

HD = 128
ROPE = 64
VD = 128
LAT = 512
HOPS = 4
MARKS = 64
FAR = 1e30
PIECES = 2
PLANE = 4
PARTS = 4
COST = 1 << 20


def from_behind(value, steps):
    count = lax.axis_size("seq")
    return lax.ppermute(value, "seq", [(source, source + steps) for source in range(count - steps)])


def attend(rows, q_nope, q_rope, q_mark, content, tails, w_uk, w_uv, out):
    scale = math.log2(math.e) / math.sqrt(HD + ROPE)
    keys = content.shape[0]
    key_pair = jnp.dot(content[...], w_uk[...], preferred_element_type=jnp.float32).astype(jnp.bfloat16)
    value_pair = jnp.dot(content[...], w_uv[...], preferred_element_type=jnp.float32).astype(jnp.bfloat16)
    causal = lax.broadcasted_iota(jnp.int32, (rows, rows), 1) <= lax.broadcasted_iota(jnp.int32, (rows, rows), 0)
    low = lax.broadcasted_iota(jnp.int32, (rows, 2 * ROPE), 1) < ROPE
    ones = jnp.ones((keys, VD), jnp.bfloat16)
    for half in range(2):
        cols = slice(half * HD, (half + 1) * HD)
        rope = jnp.where(low == (half == 0), q_rope[...], q_mark[...])
        query = jnp.concatenate([q_nope[:, cols], rope], axis=1)
        key = jnp.concatenate([key_pair[:, cols], tails[half]], axis=1)
        scores = lax.dot_general(query, key, (((1,), (1,)), ((), ())), preferred_element_type=jnp.float32)
        edge = jnp.where(causal, scores[:, keys - rows :], scores[:, :rows])
        joined = jnp.concatenate([edge, scores[:, rows : keys - rows]], axis=1)
        top = jnp.max(joined, axis=-1, keepdims=True)
        raw = jnp.exp2((joined - top) * scale).astype(jnp.bfloat16)
        near = jnp.where(causal, raw[:, :rows], jnp.bfloat16(0))
        far = jnp.where(causal, jnp.bfloat16(0), raw[:, :rows])
        weights = jnp.concatenate([far, raw[:, rows:], near], axis=1)
        value = jnp.concatenate([value_pair[:, cols], ones], axis=1)
        total = jnp.dot(weights, value, preferred_element_type=jnp.float32)
        out[:, cols] = (total[:, :VD] / total[:, VD:]).astype(jnp.bfloat16)


def attention(start, pairs, q_nope, q_rope, q_mark, content, tails, w_uk, w_uv):
    rows = q_nope.shape[0]
    width = 2 * HD * pairs
    keys = content.shape[0]
    whole = lambda *shape: pl.BlockSpec(shape, lambda i: (0,) * len(shape))
    return pl.pallas_call(
        functools.partial(attend, rows),
        out_shape=jax.ShapeDtypeStruct((rows, width), jnp.bfloat16),
        grid=(pairs,),
        in_specs=[
            pl.BlockSpec((rows, 2 * HD), lambda i: (0, i + start)),
            pl.BlockSpec((rows, 2 * ROPE), lambda i: (0, i + start)),
            whole(rows, 2 * ROPE),
            whole(keys, LAT),
            whole(2, keys, 2 * ROPE),
            pl.BlockSpec((LAT, 2 * HD), lambda i: (0, i + start)),
            pl.BlockSpec((LAT, 2 * HD), lambda i: (0, i + start)),
        ],
        out_specs=pl.BlockSpec((rows, 2 * VD), lambda i: (0, i)),
        compiler_params=pltpu.CompilerParams(
            dimension_semantics=("arbitrary",), vmem_limit_bytes=48 << 20
        ),
        cost_estimate=pl.CostEstimate(flops=COST, bytes_accessed=COST, transcendentals=0),
        name="attention",
    )(q_nope, q_rope, q_mark, content, tails, w_uk, w_uv)


def shards(q_nope, q_rope, latent, doc_ids, w_uk, w_uv, w_out):
    count, heads = lax.axis_size("seq"), lax.axis_size("head")
    position = lax.axis_index("seq")
    w_rows = w_out.T
    marks = (doc_ids[:, None] == jnp.arange(MARKS, dtype=jnp.int32)[None, :]).astype(jnp.bfloat16)
    payload = jnp.concatenate([latent, marks], axis=1)
    blocks = []
    for distance in range(HOPS, 0, -1):
        block = from_behind(payload, distance)
        blocks.append(
            jnp.concatenate(
                [block[:, : LAT + ROPE], jnp.where(position >= distance, block[:, LAT + ROPE :], jnp.bfloat16(1))],
                axis=1,
            )
        )
    blocks.append(payload)
    behind = jnp.concatenate(blocks, axis=0)
    content = behind[:, :LAT]
    key_rope, key_marks = behind[:, LAT : LAT + ROPE], behind[:, LAT + ROPE :]
    tails = jnp.stack(
        [jnp.concatenate([key_rope, key_marks], axis=1), jnp.concatenate([key_marks, key_rope], axis=1)]
    )
    q_mark = (marks - jnp.bfloat16(1)) * jnp.bfloat16(FAR)
    q_mark = jnp.concatenate([q_mark, q_mark], axis=1)
    fixed = (q_mark, content, tails)
    if count == 4 * PLANE and heads == 2:
        return paired(w_rows, q_nope, q_rope, fixed, w_uk, w_uv)
    attended = attention(0, q_nope.shape[1] // (2 * HD), q_nope, q_rope, *fixed, w_uk, w_uv)
    whole = lax.all_gather(w_rows, "seq", axis=0, tiled=True)
    share = product(attended, whole)
    return lax.psum_scatter(share, "head", scatter_dimension=1, tiled=True).astype(jnp.bfloat16)


def product(left, right):
    return lax.dot_general(left, right, (((1,), (1,)), ((), ())), preferred_element_type=jnp.float32)


def swapped(value, bit):
    return lax.ppermute(value, "seq", [(i, i ^ bit) for i in range(lax.axis_size("seq"))])


def after(value, *earlier):
    return lax.optimization_barrier((value, *earlier))[0]


def pair_up(block, across):
    two = jnp.concatenate([block, across], axis=0)
    return two, swapped(two, 1)


def owners(near):
    pairs = []
    for seq in range(lax.axis_size("seq")):
        group = seq // (2 * PLANE)
        keeper = group if near else 1 - group
        pairs.append((seq, keeper))
    return pairs


def to_owner(share, near):
    pairs = [(2 * seq + 1 - keeper, 2 * seq + keeper) for seq, keeper in owners(near)]
    return lax.ppermute(share.astype(jnp.bfloat16), ("seq", "head"), pairs).astype(jnp.float32)


def to_tokens(done, near):
    pairs = [(2 * seq + keeper, 2 * (seq ^ PLANE) + keeper) for seq, keeper in owners(near)]
    return lax.ppermute(done, ("seq", "head"), pairs)


def paired(w_rows, q_nope, q_rope, fixed, w_uk, w_uv):
    rows, width = q_nope.shape
    position, mine = lax.axis_index("seq"), lax.axis_index("head")
    plane, rank = position // PLANE, position % PLANE
    slab = w_rows.shape[0]
    step = slab // PIECES
    q_mark, content, tails = fixed
    w_rows = lax.optimization_barrier(w_rows)
    pieces = [w_rows[i * step : (i + 1) * step] for i in range(PIECES)]
    far = [swapped(pieces[0], 2 * PLANE)]
    near_across = swapped(w_rows, 2)
    each = width // (2 * HD) // PARTS

    def part(i, mark):
        return attention(i * each, each, q_nope, q_rope, mark, content, tails, w_uk, w_uv)

    own = [part(0, q_mark)]
    far.append(swapped(after(pieces[1], own[0]), 2 * PLANE))
    partner = [swapped(own[0], PLANE)]
    own.append(part(1, after(q_mark, own[0])))
    partner.append(swapped(own[1], PLANE))
    own.append(part(2, after(q_mark, own[1], near_across)))
    partner.append(swapped(own[2], PLANE))
    near_pair = pair_up(w_rows, near_across)
    own.append(part(3, after(q_mark, own[2])))
    partner.append(swapped(own[3], PLANE))
    far = [after(block, own[3]) for block in far]
    own, partner = jnp.concatenate(own, axis=1), jnp.concatenate(partner, axis=1)

    def finish(pair, near, gate):
        both = [jnp.concatenate([product(t, pair[0]), product(t, pair[1])], axis=1) for t in gate]
        sums = [(share + to_owner(share, near)).astype(jnp.bfloat16) for share in both]
        return both, sums[0], to_tokens(sums[1], near)

    shares, near_own, near_back = finish(near_pair, True, (own, partner))
    last = shares[1]
    far_own, far_back = [], []
    for piece, block in zip(pieces, far):
        pair = pair_up(block, swapped(block, 2))
        shares, one, two = finish(pair, False, (after(own, last), after(partner, last)))
        last = shares[1]
        far_own.append(one.reshape(rows, PLANE, 1, step))
        far_back.append(two.reshape(rows, PLANE, 1, step))
    keeps_near = plane // 2 == mine
    here = jnp.where(keeps_near, near_own.reshape(rows, PLANE, PIECES, step), jnp.concatenate(far_own, axis=2))
    back = jnp.where(keeps_near, near_back.reshape(rows, PLANE, PIECES, step), jnp.concatenate(far_back, axis=2))
    even = plane % 2 == 0
    both = jnp.stack([jnp.where(even, here, back), jnp.where(even, back, here)], axis=1)
    both = both.reshape(rows, 2, 2, 2, slab)
    both = jnp.where(rank % 2 == 0, both, both[:, :, ::-1])
    both = jnp.where(rank // 2 == 0, both, both[:, :, :, ::-1])
    return both.transpose(0, 1, 3, 2, 4).reshape(rows, 2 * PLANE * slab)


def solution(mesh):
    placed = (
        P("seq", "head"),
        P("seq", "head"),
        P("seq", None),
        P("seq"),
        P(None, "head"),
        P(None, "head"),
        P("head", "seq"),
    )
    return jax.shard_map(
        shards, mesh=mesh, in_specs=placed, out_specs=P("seq", "head"), check_vma=False
    )
```

```python
import functools
import math

import jax
import jax.numpy as jnp
from jax import lax
from jax.experimental import pallas as pl
from jax.experimental.pallas import tpu as pltpu
from jax.sharding import PartitionSpec as P

HD = 128
ROPE = 64
VD = 128
LAT = 512
HOPS = 4
MARKS = 64
FAR = 1e30
PLANE = 4
PARTS = 2
COST = 1 << 20


def from_behind(value, steps):
    count = lax.axis_size("seq")
    return lax.ppermute(value, "seq", [(source, source + steps) for source in range(count - steps)])


def attend(rows, q_nope, q_rope, q_mark, content, tails, w_uk, w_uv, out):
    scale = math.log2(math.e) / math.sqrt(HD + ROPE)
    keys = content.shape[0]
    key_pair = jnp.dot(content[...], w_uk[...], preferred_element_type=jnp.float32).astype(jnp.bfloat16)
    value_pair = jnp.dot(content[...], w_uv[...], preferred_element_type=jnp.float32).astype(jnp.bfloat16)
    causal = lax.broadcasted_iota(jnp.int32, (rows, rows), 1) <= lax.broadcasted_iota(jnp.int32, (rows, rows), 0)
    low = lax.broadcasted_iota(jnp.int32, (rows, 2 * ROPE), 1) < ROPE
    ones = jnp.ones((keys, VD), jnp.bfloat16)
    for half in range(2):
        cols = slice(half * HD, (half + 1) * HD)
        rope = jnp.where(low == (half == 0), q_rope[...], q_mark[...])
        query = jnp.concatenate([q_nope[:, cols], rope], axis=1)
        key = jnp.concatenate([key_pair[:, cols], tails[half]], axis=1)
        scores = lax.dot_general(query, key, (((1,), (1,)), ((), ())), preferred_element_type=jnp.float32)
        edge = jnp.where(causal, scores[:, keys - rows :], scores[:, :rows])
        joined = jnp.concatenate([edge, scores[:, rows : keys - rows]], axis=1)
        top = jnp.max(joined, axis=-1, keepdims=True)
        raw = jnp.exp2((joined - top) * scale).astype(jnp.bfloat16)
        near = jnp.where(causal, raw[:, :rows], jnp.bfloat16(0))
        far = jnp.where(causal, jnp.bfloat16(0), raw[:, :rows])
        weights = jnp.concatenate([far, raw[:, rows:], near], axis=1)
        value = jnp.concatenate([value_pair[:, cols], ones], axis=1)
        total = jnp.dot(weights, value, preferred_element_type=jnp.float32)
        out[:, cols] = (total[:, :VD] / total[:, VD:]).astype(jnp.bfloat16)


def attention(start, pairs, q_nope, q_rope, q_mark, content, tails, w_uk, w_uv):
    rows = q_nope.shape[0]
    width = 2 * HD * pairs
    keys = content.shape[0]
    whole = lambda *shape: pl.BlockSpec(shape, lambda i: (0,) * len(shape))
    return pl.pallas_call(
        functools.partial(attend, rows),
        out_shape=jax.ShapeDtypeStruct((rows, width), jnp.bfloat16),
        grid=(pairs,),
        in_specs=[
            pl.BlockSpec((rows, 2 * HD), lambda i: (0, i + start)),
            pl.BlockSpec((rows, 2 * ROPE), lambda i: (0, i + start)),
            whole(rows, 2 * ROPE),
            whole(keys, LAT),
            whole(2, keys, 2 * ROPE),
            pl.BlockSpec((LAT, 2 * HD), lambda i: (0, i + start)),
            pl.BlockSpec((LAT, 2 * HD), lambda i: (0, i + start)),
        ],
        out_specs=pl.BlockSpec((rows, 2 * VD), lambda i: (0, i)),
        compiler_params=pltpu.CompilerParams(
            dimension_semantics=("arbitrary",), vmem_limit_bytes=48 << 20
        ),
        cost_estimate=pl.CostEstimate(flops=COST, bytes_accessed=COST, transcendentals=0),
        name="attention",
    )(q_nope, q_rope, q_mark, content, tails, w_uk, w_uv)


def shards(q_nope, q_rope, latent, doc_ids, w_uk, w_uv, w_out):
    count, heads = lax.axis_size("seq"), lax.axis_size("head")
    position = lax.axis_index("seq")
    w_rows = w_out.T
    marks = (doc_ids[:, None] == jnp.arange(MARKS, dtype=jnp.int32)[None, :]).astype(jnp.bfloat16)
    payload = jnp.concatenate([latent, marks], axis=1)
    blocks = []
    for distance in range(HOPS, 0, -1):
        block = from_behind(payload, distance)
        blocks.append(
            jnp.concatenate(
                [block[:, : LAT + ROPE], jnp.where(position >= distance, block[:, LAT + ROPE :], jnp.bfloat16(1))],
                axis=1,
            )
        )
    blocks.append(payload)
    behind = jnp.concatenate(blocks, axis=0)
    content = behind[:, :LAT]
    key_rope, key_marks = behind[:, LAT : LAT + ROPE], behind[:, LAT + ROPE :]
    tails = jnp.stack(
        [jnp.concatenate([key_rope, key_marks], axis=1), jnp.concatenate([key_marks, key_rope], axis=1)]
    )
    q_mark = (marks - jnp.bfloat16(1)) * jnp.bfloat16(FAR)
    q_mark = jnp.concatenate([q_mark, q_mark], axis=1)
    fixed = (q_mark, content, tails)
    if count == 4 * PLANE and heads == 2:
        return paired(w_rows, q_nope, q_rope, fixed, w_uk, w_uv)
    attended = attention(0, q_nope.shape[1] // (2 * HD), q_nope, q_rope, *fixed, w_uk, w_uv)
    whole = lax.all_gather(w_rows, "seq", axis=0, tiled=True)
    share = product(attended, whole)
    return lax.psum_scatter(share, "head", scatter_dimension=1, tiled=True).astype(jnp.bfloat16)


def product(left, right):
    return lax.dot_general(left, right, (((1,), (1,)), ((), ())), preferred_element_type=jnp.float32)


def swapped(value, bit):
    return lax.ppermute(value, "seq", [(i, i ^ bit) for i in range(lax.axis_size("seq"))])


def after(value, *earlier):
    return lax.optimization_barrier((value, *earlier))[0]


def exchange(share, mine):
    half = share.shape[1] // 2
    first, second = share[:, :half], share[:, half:]
    keep = jnp.where(mine == 0, first, second)
    give = jnp.where(mine == 0, second, first).astype(jnp.bfloat16)
    taken = lax.ppermute(give, "head", [(0, 1), (1, 0)])
    return (keep + taken.astype(jnp.float32)).astype(jnp.bfloat16)


def paired(w_rows, q_nope, q_rope, fixed, w_uk, w_uv):
    width = q_nope.shape[1]
    mine = lax.axis_index("head")
    plane = lax.axis_index("seq") // PLANE
    groups = [
        [seq for seq in range(4 * PLANE) if seq // PLANE % 2 == parity] for parity in range(2)
    ]
    w_rows = after(w_rows, fixed[1])
    columns = lax.all_gather(w_rows, "seq", axis=0, tiled=True, axis_index_groups=groups)
    each = width // (2 * HD) // PARTS
    own, partner = [], []
    for i in range(PARTS):
        mark = after(fixed[0], own[-1]) if own else fixed[0]
        own.append(attention(i * each, each, q_nope, q_rope, mark, *fixed[1:], w_uk, w_uv))
        partner.append(swapped(own[i], PLANE))
    own, partner = jnp.concatenate(own, axis=1), jnp.concatenate(partner, axis=1)
    here = exchange(product(own, columns), mine)
    back = swapped(exchange(product(partner, columns), mine), PLANE)
    even = plane % 2 == 0
    return jnp.concatenate([jnp.where(even, here, back), jnp.where(even, back, here)], axis=1)


def solution(mesh):
    placed = (
        P("seq", "head"),
        P("seq", "head"),
        P("seq", None),
        P("seq"),
        P(None, "head"),
        P(None, "head"),
        P("head", "seq"),
    )
    return jax.shard_map(
        shards, mesh=mesh, in_specs=placed, out_specs=P("seq", "head"), check_vma=False
    )
```

```python
import functools
import math

import jax
import jax.numpy as jnp
from jax import lax
from jax.experimental import pallas as pl
from jax.experimental.pallas import tpu as pltpu
from jax.sharding import PartitionSpec as P

HD = 128
ROPE = 64
VD = 128
LAT = 512
HOPS = 4
MARKS = 64
FAR = 1e30
COST = 1 << 20


def from_behind(value, steps):
    count = lax.axis_size("seq")
    return lax.ppermute(value, "seq", [(source, source + steps) for source in range(count - steps)])


def attend(rows, q_nope, q_rope, q_mark, content, tails, w_uk, w_uv, out):
    scale = math.log2(math.e) / math.sqrt(HD + ROPE)
    keys = content.shape[0]
    key_pair = jnp.dot(content[...], w_uk[...], preferred_element_type=jnp.float32).astype(jnp.bfloat16)
    value_pair = jnp.dot(content[...], w_uv[...], preferred_element_type=jnp.float32).astype(jnp.bfloat16)
    causal = lax.broadcasted_iota(jnp.int32, (rows, rows), 1) <= lax.broadcasted_iota(jnp.int32, (rows, rows), 0)
    low = lax.broadcasted_iota(jnp.int32, (rows, 2 * ROPE), 1) < ROPE
    ones = jnp.ones((keys, VD), jnp.bfloat16)
    for half in range(2):
        cols = slice(half * HD, (half + 1) * HD)
        rope = jnp.where(low == (half == 0), q_rope[...], q_mark[...])
        query = jnp.concatenate([q_nope[:, cols], rope], axis=1)
        key = jnp.concatenate([key_pair[:, cols], tails[half]], axis=1)
        scores = lax.dot_general(query, key, (((1,), (1,)), ((), ())), preferred_element_type=jnp.float32)
        edge = jnp.where(causal, scores[:, keys - rows :], scores[:, :rows])
        joined = jnp.concatenate([edge, scores[:, rows : keys - rows]], axis=1)
        top = jnp.max(joined, axis=-1, keepdims=True)
        raw = jnp.exp2((joined - top) * scale).astype(jnp.bfloat16)
        near = jnp.where(causal, raw[:, :rows], jnp.bfloat16(0))
        far = jnp.where(causal, jnp.bfloat16(0), raw[:, :rows])
        weights = jnp.concatenate([far, raw[:, rows:], near], axis=1)
        value = jnp.concatenate([value_pair[:, cols], ones], axis=1)
        total = jnp.dot(weights, value, preferred_element_type=jnp.float32)
        out[:, cols] = (total[:, :VD] / total[:, VD:]).astype(jnp.bfloat16)


def attention(start, pairs, q_nope, q_rope, q_mark, content, tails, w_uk, w_uv):
    rows = q_nope.shape[0]
    width = 2 * HD * pairs
    keys = content.shape[0]
    whole = lambda *shape: pl.BlockSpec(shape, lambda i: (0,) * len(shape))
    return pl.pallas_call(
        functools.partial(attend, rows),
        out_shape=jax.ShapeDtypeStruct((rows, width), jnp.bfloat16),
        grid=(pairs,),
        in_specs=[
            pl.BlockSpec((rows, 2 * HD), lambda i: (0, i + start)),
            pl.BlockSpec((rows, 2 * ROPE), lambda i: (0, i + start)),
            whole(rows, 2 * ROPE),
            whole(keys, LAT),
            whole(2, keys, 2 * ROPE),
            pl.BlockSpec((LAT, 2 * HD), lambda i: (0, i + start)),
            pl.BlockSpec((LAT, 2 * HD), lambda i: (0, i + start)),
        ],
        out_specs=pl.BlockSpec((rows, 2 * VD), lambda i: (0, i)),
        compiler_params=pltpu.CompilerParams(
            dimension_semantics=("arbitrary",), vmem_limit_bytes=48 << 20
        ),
        cost_estimate=pl.CostEstimate(flops=COST, bytes_accessed=COST, transcendentals=0),
        name="attention",
    )(q_nope, q_rope, q_mark, content, tails, w_uk, w_uv)


def shards(q_nope, q_rope, latent, doc_ids, w_uk, w_uv, w_out):
    heads = lax.axis_size("head")
    position = lax.axis_index("seq")
    whole = lax.all_gather(w_out, "seq", axis=1, tiled=True)
    marks = (doc_ids[:, None] == jnp.arange(MARKS, dtype=jnp.int32)[None, :]).astype(jnp.bfloat16)
    payload = jnp.concatenate([latent, marks], axis=1)
    blocks = []
    for distance in range(HOPS, 0, -1):
        block = from_behind(payload, distance)
        blocks.append(
            jnp.concatenate(
                [block[:, : LAT + ROPE], jnp.where(position >= distance, block[:, LAT + ROPE :], jnp.bfloat16(1))],
                axis=1,
            )
        )
    blocks.append(payload)
    behind = jnp.concatenate(blocks, axis=0)
    content = behind[:, :LAT]
    key_rope, key_marks = behind[:, LAT : LAT + ROPE], behind[:, LAT + ROPE :]
    tails = jnp.stack(
        [jnp.concatenate([key_rope, key_marks], axis=1), jnp.concatenate([key_marks, key_rope], axis=1)]
    )
    q_mark = (marks - jnp.bfloat16(1)) * jnp.bfloat16(FAR)
    q_mark = jnp.concatenate([q_mark, q_mark], axis=1)
    fixed = (q_mark, content, tails)
    attended = attention(0, q_nope.shape[1] // (2 * HD), q_nope, q_rope, *fixed, w_uk, w_uv)
    share = jnp.dot(attended, whole, preferred_element_type=jnp.float32)
    if heads == 2:
        return exchange(share, lax.axis_index("head"))
    return lax.psum_scatter(share, "head", scatter_dimension=1, tiled=True).astype(jnp.bfloat16)


def exchange(share, mine):
    half = share.shape[1] // 2
    first, second = share[:, :half], share[:, half:]
    keep = jnp.where(mine == 0, first, second)
    give = jnp.where(mine == 0, second, first).astype(jnp.bfloat16)
    taken = lax.ppermute(give, "head", [(0, 1), (1, 0)])
    return (keep + taken.astype(jnp.float32)).astype(jnp.bfloat16)


def solution(mesh):
    placed = (
        P("seq", "head"),
        P("seq", "head"),
        P("seq", None),
        P("seq"),
        P(None, "head"),
        P(None, "head"),
        P("head", "seq"),
    )
    return jax.shard_map(
        shards, mesh=mesh, in_specs=placed, out_specs=P("seq", "head"), check_vma=False
    )
```
